256 devices in a mesh: row: 64 (over z, x, y_hi), layer: 4 (over y_lo, core).
Axes of the slice: x: 4, y: 4 (y_hi: 2, y_lo: 2; y = y_hi * 2 + y_lo), z: 8, core: 2. Of those that a mesh axis runs over, the one named last changes fastest.
Arguments:
- left_factor: float32 [32768, 512], P('row'), may hold values from -6 to 6
- right_factor: float32 [32768, 512], P(('row', 'layer')), may hold values from -0.25 to 0.25
- block_columns: int32 [256, 64], P('row', 'layer'), may hold values from -1 to 255, as said below
- labels: int32 [256, 64, 128, 128], P('row', 'layer'), may hold values 0 or 1
Outputs:
- left_grad: float32 [32768, 512], P('row', 'layer')
The draws below stay inside these ranges and needn't reach their ends.
Inputs may be any that keep to these rules, and one draw needn't show every extreme that they name: `block_columns`: entries l*16 to (l+1)*16 - 1 of row t list, in ascending order and each once, occupied tile columns j of tile row t with j % 4 == l, then -1 in the unused slots; every list holds at least one column, and in every draw some list of each group l is full.
All inputs are finite; a program needn't handle non-finite values. No bound on the sum of `labels` on one device may be relied on, other than what follows from the above.
Results may differ from the reference program's by a relative error of at most 0.0003.
Values sent between devices are 32-bit elements; how exact they have to be, the bound alone decides.
No kernel may reach another device: no remote copies, remote signals or barrier semaphores. Data moves between devices by JAX's collectives and lax.ppermute only.
A program may use at most 64 MiB of HBM per device.

```python
import jax
import jax.numpy as jnp
from jax import lax

K = 512
TILE = 128
SLOTS = 16
LAYERS = 4
ROWS = 32768
TROWS = 256
TCOLS = 256
NCOLS = 32768


def draw_block_columns(key, part):
    key_count, key_order, key_full = jax.random.split(key, 3)
    holders = TCOLS // LAYERS
    level = jax.random.randint(key_count, (TROWS, LAYERS), 1, SLOTS + 1)
    chosen = jax.random.randint(key_full, (LAYERS,), 0, TROWS)
    forced = lax.broadcasted_iota(jnp.int32, (TROWS, LAYERS), 0) == chosen[None, :]
    level = jnp.where(forced, SLOTS, level)
    counts = jnp.maximum(1, (level * level + level * SLOTS) // (2 * SLOTS))
    noise = jax.random.randint(key_order, (TROWS, LAYERS, holders), 0, 1 << 20)
    scores = noise * holders + lax.broadcasted_iota(jnp.int32, (TROWS, LAYERS, holders), 2)
    order = jnp.argsort(scores, axis=2, stable=True)[:, :, :SLOTS]
    order = jnp.sort(order, axis=2).astype(jnp.int32)
    slot_index = lax.broadcasted_iota(jnp.int32, (TROWS, LAYERS, SLOTS), 2)
    layer_index = lax.broadcasted_iota(jnp.int32, (TROWS, LAYERS, SLOTS), 1)
    columns = jnp.where(slot_index < counts[:, :, None], order * LAYERS + layer_index, -1)
    return columns.reshape(TROWS, LAYERS * SLOTS).astype(jnp.int32)


def set_ends(values, key, least, high):
    place = [jax.random.randint(jax.random.fold_in(key, axis), (), 0, length) for axis, length in enumerate(values.shape)]
    widest = values.shape.index(max(values.shape))
    next_to = place[:widest] + [(place[widest] + 1) % values.shape[widest]] + place[widest + 1:]
    return values.at[tuple(place)].set(least).at[tuple(next_to)].set(high)


def block_scale(own_key, dims, shards, low, high):
    def one(position, parts):
        draws = jax.random.uniform(jax.random.fold_in(jax.random.fold_in(own_key, 6), position), (parts,), jnp.float32, low / len(shards), high / len(shards))
        return jnp.repeat(jnp.exp(draws), dims[position] // parts).reshape((-1,) + (1,) * (len(dims) - position - 1))

    factor_of = one(*shards[0])
    for cut in shards[1:]:
        factor_of = factor_of * one(*cut)
    return factor_of


def bell_draw(own_key, dims, width, limit, cuts=(), dtype=jnp.bfloat16):
    values = jax.random.normal(own_key, dims, jnp.float32) * width
    if len(cuts) > 0:
        values = block_scale(own_key, dims, cuts, -0.22, 0.18) * values
    return jnp.clip(values, min=-limit, max=limit).astype(dtype)


def setup_inputs(seed: int = 0) -> dict:
    splits = jax.random.split(jax.random.key(seed), 5)
    left_factor = bell_draw(splits[0], (ROWS, K), 1.0, 6.0, ((0, 64),), jnp.float32)
    right_factor = bell_draw(splits[1], (NCOLS, K), K ** -0.5, 0.25, ((0, 256),), jnp.float32)
    block_columns = draw_block_columns(jax.random.fold_in(splits[4], 71), 0)
    labels = set_ends((jax.random.randint(splits[3], (TROWS, LAYERS * SLOTS, TILE, TILE), 0, 2) < 1).astype(jnp.int32), jax.random.fold_in(splits[3], 1), 0, 1)
    return {"left_factor": left_factor, "right_factor": right_factor, "block_columns": block_columns, "labels": labels}


shrink_rate = 0.1


def reference(left_factor, right_factor, block_columns, labels):
    right_tiles = right_factor.reshape(TCOLS, TILE, K)

    def one_row(inputs):
        left_rows, columns, targets = inputs
        occupied = (columns >= 0).astype(jnp.float32)
        picked = right_tiles[jnp.clip(columns, 0, TCOLS - 1).astype(jnp.int32)]
        scores = jnp.einsum("ak,sbk->sab", left_rows, picked, precision=lax.Precision.HIGHEST)
        residue = (jax.nn.sigmoid(scores) - targets.astype(jnp.float32)) * occupied[:, None, None]
        return jnp.einsum("sab,sbk->ak", residue, picked, precision=lax.Precision.HIGHEST)

    gradient = lax.map(one_row, (left_factor.reshape(TROWS, TILE, K), block_columns, labels))
    return gradient.reshape(ROWS, K) + shrink_rate * left_factor
```

```python
import functools

import jax
import jax.numpy as jnp
import numpy as np
from jax import lax
from jax.experimental import pallas as pl
from jax.experimental.pallas import tpu as pltpu
from jax.sharding import PartitionSpec as P

shrink_rate = 0.1

NZ, NX, NY = 8, 4, 2
VMEM = pltpu.VMEM


def holder_of(z, x, y):
    return (z * NX + x) * NY + y


def row_pairs(dz, dx, dy):
    return [
        (holder_of(z, x, y), holder_of((z + dz) % NZ, (x + dx) % NX, (y + dy) % NY))
        for z in range(NZ)
        for x in range(NX)
        for y in range(NY)
    ]


def shift(value, dz=0, dx=0, dy=0):
    return lax.ppermute(value, "row", row_pairs(dz, dx, dy))


def split_kernel(x_ref, out_ref):
    for tile in range(x_ref.shape[0]):
        value = x_ref[tile]
        high = value.astype(jnp.bfloat16)
        out_ref[tile, 0:128] = high
        out_ref[tile, 128:256] = (value - high.astype(jnp.float32)).astype(jnp.bfloat16)


def split_rows(left):
    return pl.pallas_call(
        split_kernel,
        out_shape=jax.ShapeDtypeStruct((left.shape[0], 256, left.shape[2]), jnp.bfloat16),
        in_specs=[pl.BlockSpec(memory_space=VMEM)],
        out_specs=pl.BlockSpec(memory_space=VMEM),
        compiler_params=pltpu.CompilerParams(vmem_limit_bytes=4 << 20),
    )(left)


def visit_kernel(groups, first, has_total, slots_ref, left_ref, labels_ref, *refs):
    count = sum(len(group) for group in groups)
    value_refs, refs = refs[:count], refs[count:]
    if has_total:
        refs = refs[1:]
    total_ref, held_ref = refs
    tile_rows = left_ref.shape[0]
    if not has_total:
        total_ref[...] = jnp.zeros_like(total_ref)

    def entry(tile, index):
        slot = slots_ref[tile, index]

        @pl.when(slot >= 0)
        def _():
            parts = lax.dot_general(
                left_ref[tile],
                held_ref[...],
                (((1,), (1,)), ((), ())),
                preferred_element_type=jnp.float32,
            )
            scores = (parts[0:128, 0:128] + parts[128:256, 128:256]) + (
                parts[0:128, 128:256] + parts[128:256, 0:128]
            )
            residue = 1.0 / (1.0 + jnp.exp(-scores)) - labels_ref[tile, slot].astype(jnp.float32)
            high = residue.astype(jnp.bfloat16)
            low = (residue - high.astype(jnp.float32)).astype(jnp.bfloat16)
            spread = jnp.concatenate(
                [jnp.concatenate([high, high], axis=1), jnp.concatenate([low, low], axis=1)], axis=0
            )
            update = jnp.dot(spread, held_ref[...], preferred_element_type=jnp.float32)
            total_ref[tile] += update[0:128] + update[128:256]

    base, at = first, 0
    for group in groups:
        members = value_refs[at : at + len(group)]
        at += len(group)
        blocks = members[0].shape[0]

        def block(b, carry, members=members, base=base):
            index = base + b
            wanted = slots_ref[0, index]
            for tile in range(1, tile_rows):
                wanted = jnp.maximum(wanted, slots_ref[tile, index])

            @pl.when(wanted >= 0)
            def _():
                row = 0
                for ref in members:
                    rows = ref.shape[1]
                    value = ref[b]
                    high = value.astype(jnp.bfloat16)
                    held_ref[row : row + rows] = high
                    held_ref[128 + row : 128 + row + rows] = (
                        value - high.astype(jnp.float32)
                    ).astype(jnp.bfloat16)
                    row += rows

                def one(tile, c):
                    entry(tile, index)
                    return c

                lax.fori_loop(0, tile_rows, one, 0)

            return carry

        lax.fori_loop(0, blocks, block, 0)
        base += blocks


def visit(groups, first, slots, left, labels, total):
    values = [v for group in groups for v in group]
    has_total = total is not None
    blocks = sum(group[0].shape[0] for group in groups)
    shape = (left.shape[0], 128, left.shape[2])
    operands = [slots, left, labels, *values] + ([total] if has_total else [])
    return pl.pallas_call(
        functools.partial(
            visit_kernel, [tuple(range(len(group))) for group in groups], first, has_total
        ),
        out_shape=jax.ShapeDtypeStruct(shape, jnp.float32),
        in_specs=[pl.BlockSpec(memory_space=pltpu.SMEM)]
        + [pl.BlockSpec(memory_space=VMEM)] * (len(operands) - 1),
        out_specs=pl.BlockSpec(memory_space=VMEM),
        scratch_shapes=[VMEM((256, left.shape[2]), jnp.bfloat16)],
        input_output_aliases={len(operands) - 1: 0} if has_total else {},
        cost_estimate=pl.CostEstimate(
            flops=blocks * 300_000_000, bytes_accessed=blocks * 262144, transcendentals=0
        ),
        compiler_params=pltpu.CompilerParams(vmem_limit_bytes=4 << 20),
    )(*operands)


def per_device(left_factor, right_factor, block_columns, labels):
    row_index = lax.axis_index("row")
    layer_index = lax.axis_index("layer")
    z, x, y = row_index // (NX * NY), (row_index // NY) % NX, row_index % NY
    x_groups = [[holder_of(zz, xx, yy) for xx in range(NX)] for zz in range(NZ) for yy in range(NY)]

    tile_rows = block_columns.shape[0]
    left = split_rows(left_factor.reshape(tile_rows, 128, left_factor.shape[1]))

    partner = shift(right_factor, dy=1)
    own = lax.all_to_all(
        jnp.broadcast_to(right_factor[None], (NX, *right_factor.shape)),
        "row",
        0,
        0,
        axis_index_groups=x_groups,
    )

    half = right_factor.shape[0] // 2

    def line(dz):
        return [(dz, xx, True) for xx in range(NX)]

    def ring(value, dim, n):
        up, down = [value], [value]
        for _ in range(n // 2 - 1):
            up.append(shift(up[-1], **{dim: 1}))
            down.append(shift(down[-1], **{dim: -1}))
        last_up = shift(up[-1][:, :half], **{dim: 1})
        last_down = shift(down[-1][:, half:], **{dim: -1})
        return up[1:], down[1:], (last_up, last_down)

    b_up, b_down, b_last = ring(partner[None], "dz", NZ)
    a_up, a_down, a_last = ring(own, "dz", NZ)
    near = jnp.concatenate([partner[None], b_up[0], b_down[0]], axis=0)
    near_z = [0, -1, 1]
    rest = jnp.concatenate(
        [b_up[1], b_down[1], b_up[2], b_down[2], jnp.concatenate(b_last, axis=1)], axis=0
    )
    rest_z = [-2, 2, -3, 3, 4]

    def column(zs, dx):
        return [(dz, dx, False) for dz in zs]

    n_up, n_down, n_last = ring(near, "dx", NX)
    r_up, r_down, r_last = ring(rest, "dx", NX)

    calls = [
        [((own,), line(0))],
        [((near,), column(near_z, 0))],
        [((a_up[0],), line(-1)), ((a_down[0],), line(1))],
        [((rest,), column(rest_z, 0))],
        [((n_up[0],), column(near_z, -1)), ((n_down[0],), column(near_z, 1))],
        [((a_up[1],), line(-2)), ((a_down[1],), line(2))],
        [(n_last, column(near_z, 2))],
        [((r_up[0],), column(rest_z, -1)), ((r_down[0],), column(rest_z, 1))],
        [((a_up[2],), line(-3)), ((a_down[2],), line(3))],
        [(r_last, column(rest_z, 2))],
        [(a_last, line(4))],
    ]
    places = np.array([p for call in calls for _, places in call for p in places], np.int32)
    same = places[:, 2]
    order = holder_of(
        (z + places[:, 0]) % NZ, (x * (1 - same) + places[:, 1]) % NX, y + (1 - 2 * y) * (1 - same)
    )
    wanted = order * 4 + layer_index
    slot_iota = lax.broadcasted_iota(jnp.int32, (1, block_columns.shape[1], 1), 1)
    slots = jnp.max(
        jnp.where(block_columns[:, :, None] == wanted[None, None, :], slot_iota, -1), axis=1
    )

    total, first = None, 0
    for call in calls:
        total = visit([group for group, _ in call], first, slots, left, labels, total)
        first += sum(len(places) for _, places in call)
    total = total.reshape(left_factor.shape)

    width = left_factor.shape[1] // 4
    core, low = layer_index % 2, layer_index // 2
    cores = [(r * 4 + l, r * 4 + (l ^ 1)) for r in range(64) for l in range(4)]
    lows = [(r * 4 + l, r * 4 + (l ^ 2)) for r in range(64) for l in range(4)]
    parts = total.reshape(total.shape[0], 2, 2, width)

    def pick(array, axis, index):
        return lax.dynamic_index_in_dim(array, index, axis, keepdims=False)

    mine = pick(parts, 2, core) + lax.ppermute(pick(parts, 2, 1 - core), ("row", "layer"), cores)
    shared = pick(mine, 1, low) + lax.ppermute(pick(mine, 1, 1 - low), ("row", "layer"), lows)
    own_part = lax.dynamic_slice_in_dim(left_factor, layer_index * width, width, 1)
    return shared + shrink_rate * own_part


def solution(mesh):
    in_specs = (
        P("row", None),
        P(("row", "layer"), None),
        P("row", "layer"),
        P("row", "layer", None, None),
    )
    return jax.shard_map(
        per_device, mesh=mesh, in_specs=in_specs, out_specs=P("row", "layer"), check_vma=False
    )
```
